32 devices in a mesh: layer: 2 (over z_hi), latent: 8 (over y, x, core), dp: 2 (over z_lo).
Axes of the slice: x: 2, y: 2, z: 4 (z_hi: 2, z_lo: 2; z = z_hi * 2 + z_lo), core: 2. Of those that a mesh axis runs over, the one named last changes fastest.
Arguments:
- layer_acts: bfloat16 [2, 128, 2560], P('layer', ('latent', 'dp')), may hold values from -6 to 6
- enc_weight: bfloat16 [2, 2560, 2048], P('layer', None, 'latent'), may hold values from -0.078125 to 0.078125
- dec_weight: bfloat16 [2, 2048, 2560], P('layer', 'latent'), may hold values from -0.125 to 0.125
- enc_bias: float32 [2048], P('latent'), may hold values from -3 to 3
- dec_bias: float32 [2, 2560], P('layer'), may hold values from -3 to 3
- block_ids: int32 [8, 16, 2], P('latent'), may hold values from 0 to 1, as said below
- block_counts: int32 [8, 16], P('latent'), may hold values from 1 to 2, as said below
Outputs:
- enc_grad: bfloat16 [2, 2560, 2048], P('layer', 'dp', 'latent')
- dec_grad: bfloat16 [2, 2048, 2560], P('layer', 'latent', 'dp')
- enc_bias_grad: float32 [2048], P(('latent', 'dp'))
- dec_bias_grad: float32 [2, 2560], P('layer', 'dp')
The draws below stay inside these ranges and needn't reach their ends.
Inputs may be any that keep to these rules, and one draw needn't show every extreme that they name: block_ids[s, t] holds each of 0 .. 1 once. `block_counts`: every latent shard has a row tile with all 2 blocks active and one with a single active block.
All inputs are finite; a program needn't handle non-finite values.
Results may differ from the reference program's by a relative error of at most 0.02.
Values may be sent and summed in bfloat16 or wider, within the bound.
A program may use at most 64 MiB of HBM per device.

```python
import math
import jax
import jax.numpy as jnp
from jax import lax

D = 2560
BLOCK = 128
BLK_DEV = 2
ROWS_DEV = 8
LAT_DEV = 256
SHARDS = 8
LATENTS = 2048
LAYERS = 2
TILES = 16
ROWS_DP = 64
ROWS = 128
N_LATENT = 8
N_DP = 2


def draw_block_ids(key, part):
    scores = jax.random.randint(jax.random.fold_in(key, 11), (SHARDS, TILES, BLK_DEV), 0, 1 << 20)
    scores = scores * BLK_DEV + jnp.arange(BLK_DEV, dtype=jnp.int32)[None, None, :]
    return jnp.argsort(scores, axis=-1, stable=True).astype(jnp.int32)


def draw_block_counts(key, part):
    base = jax.random.randint(jax.random.fold_in(key, 21), (SHARDS, TILES), 1, BLK_DEV + 1)
    full_tile = jax.random.randint(jax.random.fold_in(key, 22), (SHARDS, 1), 0, TILES)
    tile_index = jnp.arange(TILES, dtype=jnp.int32)[None, :]
    single_tile = (full_tile + 1) % TILES
    counts = jnp.where(tile_index == full_tile, BLK_DEV, jnp.where(tile_index == single_tile, 1, base))
    return counts.astype(jnp.int32)


def levels(own_key, extent, cuts, low, high):
    gain, own = 1.0, jax.random.fold_in(own_key, 6)
    for position, parts in cuts:
        heights = jnp.exp(jax.random.uniform(jax.random.fold_in(own, position), (parts,), jnp.float32, low / len(cuts), high / len(cuts)))
        gain = gain * jnp.repeat(heights, extent[position] // parts).reshape([-1 if axis == position else 1 for axis in range(len(extent))])
    return gain


def scatter_about(stream_key, shape, scale, most, shards=(), kind=jnp.bfloat16):
    drawn = scale * jax.random.normal(stream_key, shape, jnp.float32)
    if shards:
        drawn = drawn * levels(stream_key, shape, shards, -0.22, 0.18)
    return jnp.clip(drawn, -most, most).astype(kind)


def setup_inputs(seed: int = 0) -> dict:
    key_of = jax.random.split(jax.random.key(seed), 8)
    return {
        "layer_acts": scatter_about(key_of[0], (LAYERS, ROWS, D), 1.0, 6.0, ((0, 2), (1, 16))),
        "enc_weight": scatter_about(key_of[1], (LAYERS, D, LATENTS), (D * LAYERS) ** -0.5, 0.078125, ((0, 2), (2, 8))),
        "dec_weight": scatter_about(key_of[2], (LAYERS, LATENTS, D), LATENTS ** -0.5, 0.125, ((0, 2), (1, 8))),
        "enc_bias": scatter_about(key_of[3], (LATENTS,), 0.5, 3.0, ((0, 8),), jnp.float32),
        "dec_bias": scatter_about(key_of[4], (LAYERS, D), 0.5, 3.0, ((0, 2),), jnp.float32),
        "block_ids": draw_block_ids(jax.random.fold_in(key_of[7], 71), 0),
        "block_counts": draw_block_counts(jax.random.fold_in(key_of[7], 71), 0),
    }


SPARSITY = 0.5
NORM_EPS = 1e-06

def to_wire(values):
    return lax.optimization_barrier(values.astype(jnp.bfloat16)).astype(jnp.float32)

def group_rows(values):
    trailing = values.shape[-1]
    return values.reshape(N_LATENT, N_DP, ROWS_DEV, trailing).transpose(1, 0, 2, 3).reshape(N_DP, ROWS_DP, trailing)

def reference(layer_acts, enc_weight, dec_weight, enc_bias, dec_bias, block_ids, block_counts):
    grad_scale = 1.0 / math.sqrt(ROWS)
    block_slot = jnp.arange(BLK_DEV, dtype=jnp.int32)
    listed = (block_ids[:, :, :, None] == block_slot[None, None, None, :]) & (block_slot[None, None, :, None] < block_counts[:, :, None, None])
    active = jnp.any(listed, axis=2).astype(jnp.float32)
    tiled = jnp.transpose(active, (1, 0, 2))
    code_mask = jnp.broadcast_to(tiled[:, None, :, :, None], (TILES, ROWS_DEV, SHARDS, BLK_DEV, BLOCK)).reshape(ROWS, LATENTS)
    pre = jnp.zeros((ROWS, LATENTS), jnp.float32) + enc_bias[None, :]
    for layer in range(LAYERS):
        pre = pre + jnp.dot(layer_acts[layer], enc_weight[layer], preferred_element_type=jnp.float32)
    codes = (jax.nn.softplus(pre) * code_mask).astype(jnp.bfloat16)
    codes_sharded = codes.reshape(ROWS, SHARDS, LAT_DEV).transpose(1, 0, 2)
    err_list = []
    norm_list = []
    for layer in range(LAYERS):
        dec_sharded = dec_weight[layer].reshape(SHARDS, LAT_DEV, D)

        def add_shard(total, pair):
            shard_codes, shard_dec = pair
            return (total + to_wire(jnp.dot(shard_codes, shard_dec, preferred_element_type=jnp.float32)), None)
        recon, unused = lax.scan(add_shard, jnp.zeros((ROWS, D), jnp.float32), (codes_sharded, dec_sharded))
        recon = recon + dec_bias[layer][None, :]
        err_list.append((grad_scale * (recon - layer_acts[layer].astype(jnp.float32))).astype(jnp.bfloat16))
        norm_list.append(jnp.sqrt(lax.optimization_barrier(jnp.sum(jnp.square(dec_weight[layer].astype(jnp.float32)), axis=1)) + NORM_EPS))
    code_grad = jnp.zeros((ROWS, LATENTS), jnp.float32)
    for layer in range(LAYERS):
        code_grad = code_grad + lax.dot_general(err_list[layer], dec_weight[layer], (((1,), (1,)), ((), ())), preferred_element_type=jnp.float32)
        code_grad = code_grad + SPARSITY * grad_scale * norm_list[layer][None, :]
    pre_grad = (code_grad * code_mask * jax.nn.sigmoid(pre)).astype(jnp.bfloat16)
    pre_grad_groups = group_rows(pre_grad)
    codes_groups = group_rows(codes)
    code_totals = lax.optimization_barrier(jnp.sum(codes_groups.astype(jnp.float32), axis=1))
    enc_bias_grad = lax.optimization_barrier(jnp.sum(to_wire(lax.optimization_barrier(jnp.sum(pre_grad_groups.astype(jnp.float32), axis=1))), axis=0))
    enc_list = []
    dec_list = []
    bias_list = []
    for layer in range(LAYERS):
        acts_groups = group_rows(layer_acts[layer])
        err_groups = group_rows(err_list[layer])
        unit_rows = dec_weight[layer].astype(jnp.float32) / norm_list[layer][:, None]
        enc_total = jnp.zeros((D, LATENTS), jnp.float32)
        dec_total = jnp.zeros((LATENTS, D), jnp.float32)
        bias_total = jnp.zeros((D,), jnp.float32)
        for group in range(N_DP):
            enc_part = lax.dot_general(acts_groups[group], pre_grad_groups[group], (((0,), (0,)), ((), ())), preferred_element_type=jnp.float32)
            enc_total = enc_total + to_wire(enc_part)
            dec_part = lax.dot_general(codes_groups[group], err_groups[group], (((0,), (0,)), ((), ())), preferred_element_type=jnp.float32)
            dec_part = dec_part + SPARSITY * grad_scale * code_totals[group][:, None] * unit_rows
            dec_total = dec_total + to_wire(dec_part)
            bias_total = bias_total + to_wire(lax.optimization_barrier(jnp.sum(err_groups[group].astype(jnp.float32), axis=0)))
        enc_list.append(enc_total.astype(jnp.bfloat16))
        dec_list.append(dec_total.astype(jnp.bfloat16))
        bias_list.append(bias_total)
    return (jnp.stack(enc_list), jnp.stack(dec_list), enc_bias_grad, jnp.stack(bias_list))
```

```python
import functools
import math

import jax
import jax.numpy as jnp
from jax import lax
from jax.experimental import pallas as pl
from jax.experimental.pallas import tpu as pltpu
from jax.sharding import PartitionSpec as P

SPARSITY = 0.5
NORM_EPS = 1e-06
MESH = pl.DeviceIdType.MESH
F32 = jnp.float32
BF16 = jnp.bfloat16
ENC_CHUNKS = 4
SPLITS = 1
CORES = 2


def far_first(index, size):
    if size & (size - 1):
        return [lax.rem(index + k, size) for k in range(1, size)]
    peers = []
    for k in sorted(range(1, size), key=lambda k: (-bin(k).count("1"), -k)):
        peer = index
        for b in range(size.bit_length() - 1):
            if k >> b & 1:
                peer = peer + (1 << b) - (2 << b) * lax.rem(index // (1 << b), 2)
        peers.append(peer)
    return peers


def step_kernel(
    n_layer, n_lat, n_dp,
    acts_hbm, enc_hbm, dec_hbm, ebias_hbm, dbias_hbm, ids_hbm, counts_hbm,
    acts_t, pg_out, dec_stage, eb_stage, db_stage,
    acts_all, enc_v, dec_v, ebias_v, dbias_v, ids_v, counts_v,
    acts_half, pre_send, pre_recv, codes_send, codes_recv,
    part_send, pair_recv, chip_send, part_recv, err_all, err_half, grad_send, grad_recv,
    gate_send, gate_recv,
    in_sems, acts_ss, acts_rs, ahalf_ss, ahalf_rs, pre_ss, pre_rs, codes_ss, codes_rs,
    pair_ss, pair_rs, part_ss, part_rs, err_ss, err_rs, ehalf_ss, ehalf_rs, grad_ss, grad_rs, gate_ss, gate_rs,
):
    layer = lax.axis_index("layer")
    me = lax.axis_index("latent")
    group = lax.axis_index("dp")
    rows = acts_all.shape[1]
    width = acts_all.shape[2]
    lat = enc_v.shape[1]
    blocks, tiles = ids_v.shape
    rows_group = rows * n_lat
    half = width // n_dp
    lat_part = lat // n_dp
    splits = acts_rs.shape[1]
    step = width // splits
    cuts = [slice(c * step, (c + 1) * step) for c in range(splits)]
    scale = 1.0 / math.sqrt(rows_group * n_dp)

    chips = n_lat // CORES
    chip = me // CORES
    core = lax.rem(me, CORES)
    partner = chip * CORES + 1 - core
    chip_peers = far_first(chip, chips)
    lat_peers = [lax.rem(me + k, n_lat) for k in range(1, n_lat)]
    layer_peers = [lax.rem(layer + k, n_layer) for k in range(1, n_layer)]
    dp_peers = [lax.rem(group + k, n_dp) for k in range(1, n_dp)]
    z_peers = [(p, d) for p in layer_peers for d in dp_peers]
    z_peers += [(p, group) for p in layer_peers] + [(layer, d) for d in dp_peers]

    own_acts = pltpu.make_async_copy(acts_hbm.at[0], acts_all.at[me], in_sems.at[0])
    own_acts.start()
    loads = [
        pltpu.make_async_copy(src, dst, in_sems.at[i + 1])
        for i, (src, dst) in enumerate(
            (
                (enc_hbm.at[0], enc_v),
                (dec_hbm.at[0], dec_v),
                (ebias_hbm, ebias_v),
                (dbias_hbm, dbias_v),
                (ids_hbm.at[0], ids_v),
                (counts_hbm, counts_v),
            )
        )
    ]
    for load in loads:
        load.start()

    barrier = pltpu.get_barrier_semaphore()
    for p in lat_peers:
        pl.semaphore_signal(barrier, inc=1, device_id={"latent": p}, device_id_type=MESH)
    for p, d in z_peers:
        pl.semaphore_signal(barrier, inc=1, device_id={"layer": p, "dp": d}, device_id_type=MESH)
    pl.semaphore_wait(barrier, len(lat_peers) + len(z_peers))

    def remote(src, dst, ss, rs, axis, peer):
        return pltpu.make_async_remote_copy(
            src_ref=src, dst_ref=dst, send_sem=ss, recv_sem=rs,
            device_id={axis: peer}, device_id_type=MESH,
        )

    sent = []

    def send(*args):
        copy = remote(*args)
        copy.start()
        sent.append(copy)

    def share(src, buf, ss, rs, c):
        dst = buf.at[me, :, cuts[c]]
        for k, q in enumerate(chip_peers):
            send(src, dst, ss.at[k, c], rs.at[me, c], "latent", q * CORES + core)
        send(src, dst, ss.at[chips - 1, c], rs.at[me, c], "latent", partner)

    def wait_cut(buf, ss, rs, j, c):
        part = buf.at[j, :, cuts[c]]
        remote(part, part, ss.at[0, c], rs.at[j, c], "latent", partner).wait_recv()

    def pass_on(buf, ss, rs, c):
        for k, q in enumerate(chip_peers):
            j = q * CORES + core
            wait_cut(buf, ss, rs, j, c)
            part = buf.at[j, :, cuts[c]]
            send(part, part, ss.at[chips + k, c], rs.at[j, c], "latent", partner)

    def gather_cuts(buf, ss, rs, beside):
        for c in range(splits):
            pass_on(buf, ss, rs, c)
        beside()
        for c, cut in enumerate(cuts):
            wait_cut(buf, ss, rs, partner, c)
            for q in chip_peers:
                wait_cut(buf, ss, rs, q * CORES + 1 - core, c)
            yield cut, buf[:, :, cut].astype(F32).reshape(rows_group, step).astype(BF16)

    def cross(src, dst_half, ss, rs):
        for q, p in enumerate(dp_peers):
            cols = pl.ds(pl.multiple_of(p * half, 128), half)
            send(src.at[:, cols], dst_half.at[group, me], ss.at[q, 0], rs.at[group, me], "dp", p)

    own_acts.wait()
    for c, cut in enumerate(cuts):
        share(acts_all.at[me, :, cut], acts_all, acts_ss, acts_rs, c)
    cross(acts_all.at[me], acts_half, ahalf_ss, ahalf_rs)

    for load in loads:
        load.wait()
    dec_f = dec_v[...].astype(F32)
    norm_col = jnp.sqrt(jnp.sum(dec_f * dec_f, axis=1, keepdims=True) + NORM_EPS)
    r_i = lax.broadcasted_iota(jnp.int32, (lat, lat), 0)
    c_i = lax.broadcasted_iota(jnp.int32, (lat, lat), 1)
    norm_row = jnp.sum(
        jnp.where(r_i == c_i, jnp.broadcast_to(norm_col, (lat, lat)), 0.0), axis=0, keepdims=True
    )
    ids_i = ids_v[...]
    counts_i = counts_v[...]
    lat_block = lax.broadcasted_iota(jnp.int32, (rows_group, lat), 1) // (lat // blocks)
    pick_r = lax.broadcasted_iota(jnp.int32, (rows_group, tiles), 0) // rows
    pick_c = lax.broadcasted_iota(jnp.int32, (rows_group, tiles), 1)
    picked = pick_c == pick_r * n_dp + group
    mask = jnp.zeros((rows_group, lat), F32)
    for b in range(blocks):
        hit = jnp.zeros((1, tiles), F32)
        for k in range(blocks):
            hit = jnp.where((ids_i[k : k + 1, :] == b) & (counts_i > k), 1.0, hit)
        row_hit = jnp.sum(
            jnp.where(picked, jnp.broadcast_to(hit, (rows_group, tiles)), 0.0), axis=1, keepdims=True
        )
        mask = jnp.where(lat_block == b, jnp.broadcast_to(row_hit, (rows_group, lat)), mask)

    def wait_half(dst_half, ss, rs, p, j):
        remote(
            dst_half.at[p, j], dst_half.at[p, j], ss.at[0, 0], rs.at[p, j], "latent", lat_peers[0]
        ).wait_recv()

    def spread(dst_half, ss, rs):
        for q, p in enumerate(dp_peers):
            wait_half(dst_half, ss, rs, p, me)
            for k, j in enumerate(lat_peers):
                send(dst_half.at[p, me], dst_half.at[p, me], ss.at[q, k + 1], rs.at[p, me], "latent", j)

    pre = jnp.zeros((rows_group, lat), F32)
    for cut, gathered in gather_cuts(acts_all, acts_ss, acts_rs, lambda: None):
        pre = pre + jnp.dot(gathered, enc_v[cut, :], preferred_element_type=F32)
    pre_send[...] = pre.astype(BF16)
    for k, p in enumerate(layer_peers):
        send(pre_send, pre_recv.at[layer], pre_ss.at[k], pre_rs.at[layer], "layer", p)
    spread(acts_half, ahalf_ss, ahalf_rs)
    pre = pre + ebias_v[...][None, :]
    for k, p in enumerate(layer_peers):
        remote(pre_send, pre_recv.at[p], pre_ss.at[k], pre_rs.at[p], "layer", p).wait_recv()
        pre = pre + pre_recv[p].astype(F32)

    codes = (jax.nn.softplus(pre) * mask).astype(BF16)
    codes_send[...] = codes
    def reduce_pair(c):
        cut = cuts[c]
        theirs = pair_recv.at[:, :, cut]
        remote(theirs, theirs, pair_ss.at[c], pair_rs.at[c], "latent", partner).wait_recv()
        total = part_send[core, :, :, cut].astype(F32) + pair_recv[:, :, cut].astype(F32)
        chip_send[:, :, cut] = total.astype(BF16)
        for k, q in enumerate(chip_peers):
            send(
                chip_send.at[q, :, cut], part_recv.at[chip, :, cut],
                part_ss.at[k, c], part_rs.at[chip, c], "latent", q * CORES + core,
            )

    for c, cut in enumerate(cuts):
        part = jnp.dot(codes, dec_v[:, cut], preferred_element_type=F32)
        part = part.reshape(chips, CORES, rows, step).astype(BF16)
        for d in range(CORES):
            part_send[d, :, :, cut] = part[:, d]
        send(
            part_send.at[1 - core, :, :, cut], pair_recv.at[:, :, cut],
            pair_ss.at[c], pair_rs.at[c], "latent", partner,
        )
        if c > 0:
            reduce_pair(c - 1)
    reduce_pair(splits - 1)
    for k, p in enumerate(dp_peers):
        send(codes_send, codes_recv.at[group], codes_ss.at[k], codes_rs.at[group], "dp", p)

    mine_cols = pl.ds(pl.multiple_of(group * half, 128), half)
    acts_rows = [acts_all[:, :, mine_cols].astype(F32).reshape(rows_group, half)]
    for q, p in enumerate(dp_peers):
        for j in lat_peers:
            wait_half(acts_half, ahalf_ss, ahalf_rs, p, j)
        acts_rows.append(acts_half[p].astype(F32).reshape(rows_group, half))
    acts_t[...] = jnp.concatenate(acts_rows, axis=0).T.astype(BF16)

    gate = mask * jax.nn.sigmoid(pre)
    gate_send[...] = gate.astype(BF16)
    for k, p in enumerate(dp_peers):
        send(gate_send, gate_recv.at[group], gate_ss.at[k], gate_rs.at[group], "dp", p)

    for c, cut in enumerate(cuts):
        recon = part_send[core, chip, :, cut].astype(F32) + pair_recv[chip, :, cut].astype(F32)
        for q in chip_peers:
            wait_cut(part_recv, part_ss, part_rs, q, c)
            recon = recon + part_recv[q, :, cut].astype(F32)
        recon = recon + dbias_v[:, cut]
        err_all[me, :, cut] = (scale * (recon - acts_all[me, :, cut].astype(F32))).astype(BF16)
        share(err_all.at[me, :, cut], err_all, err_ss, err_rs, c)
    cross(err_all.at[me], err_half, ehalf_ss, ehalf_rs)

    code_rows = [codes.astype(F32)]
    for k, p in enumerate(dp_peers):
        remote(codes_send, codes_recv.at[p], codes_ss.at[k], codes_rs.at[p], "dp", p).wait_recv()
        code_rows.append(codes_recv[p].astype(F32))
    codes_t = jnp.concatenate(code_rows, axis=0).T
    totals = jnp.sum(codes_t, axis=1, keepdims=True)
    unit_gain = SPARSITY * scale * totals / norm_col
    codes_t = codes_t.astype(BF16)

    grad = jnp.zeros((rows_group, lat), F32)
    for cut, err in gather_cuts(err_all, err_ss, err_rs, lambda: spread(err_half, ehalf_ss, ehalf_rs)):
        grad = grad + lax.dot_general(
            err, dec_v[:, cut], (((1,), (1,)), ((), ())), preferred_element_type=F32
        )
    grad = grad + SPARSITY * scale * norm_row
    grad_send[...] = grad.astype(BF16)
    for k, (p, d) in enumerate(z_peers):
        copy = pltpu.make_async_remote_copy(
            src_ref=grad_send, dst_ref=grad_recv.at[layer, group],
            send_sem=grad_ss.at[k], recv_sem=grad_rs.at[layer, group],
            device_id={"layer": p, "dp": d}, device_id_type=MESH,
        )
        copy.start()
        sent.append(copy)

    err_rows = [err_all[:, :, mine_cols].astype(F32).reshape(rows_group, half)]
    for q, p in enumerate(dp_peers):
        for j in lat_peers:
            wait_half(err_half, ehalf_ss, ehalf_rs, p, j)
        err_rows.append(err_half[p].astype(F32).reshape(rows_group, half))
    err_rows = jnp.concatenate(err_rows, axis=0)
    db_stage[...] = jnp.sum(err_rows, axis=0, keepdims=True)
    dec_grad = jnp.dot(codes_t, err_rows.astype(BF16), preferred_element_type=F32)
    dec_grad = dec_grad + unit_gain * dec_v[:, mine_cols].astype(F32)
    dec_stage[...] = dec_grad.astype(BF16)

    gates = [gate]
    for k, d in enumerate(dp_peers):
        remote(gate_send, gate_recv.at[d], gate_ss.at[k], gate_rs.at[d], "dp", d).wait_recv()
        gates.append(gate_recv[d].astype(F32))

    def wait_grad(p, d):
        remote(grad_send, grad_recv.at[p, d], grad_ss.at[0], grad_rs.at[p, d], "latent", partner).wait_recv()
        return grad_recv[p, d].astype(F32)

    for p in layer_peers:
        grad = grad + wait_grad(p, group)
    pg_rows = [(grad * gates[0]).astype(BF16)]
    for k, d in enumerate(dp_peers):
        other = wait_grad(layer, d)
        for p in layer_peers:
            other = other + wait_grad(p, d)
        pg_rows.append((other * gates[k + 1]).astype(BF16))
    pg_rows = jnp.concatenate(pg_rows, axis=0)
    pg_out[...] = pg_rows
    bias_sum = jnp.sum(pg_rows.astype(F32), axis=0, keepdims=True)
    bias_mine = bias_sum[:, :lat_part]
    for d in range(1, n_dp):
        bias_mine = jnp.where(group == d, bias_sum[:, d * lat_part : (d + 1) * lat_part], bias_mine)
    eb_stage[...] = bias_mine.reshape(lat_part)
    for copy in sent:
        copy.wait_send()


def finish_kernel(
    acts_t, pg_rows, dec_grad, eb_grad, db_grad, enc_out, dec_out, eb_out, db_out, enc_stage, sems
):
    copies = [
        pltpu.make_async_copy(dec_grad, dec_out.at[0], sems.at[0]),
        pltpu.make_async_copy(eb_grad, eb_out, sems.at[1]),
        pltpu.make_async_copy(db_grad, db_out, sems.at[2]),
    ]
    for copy in copies:
        copy.start()
    size = acts_t.shape[0] // ENC_CHUNKS
    for c in range(ENC_CHUNKS):
        part = pl.ds(c * size, size)
        enc_stage[part, :] = jnp.dot(
            acts_t[part, :], pg_rows[...], preferred_element_type=F32
        ).astype(BF16)
        copy = pltpu.make_async_copy(enc_stage.at[part, :], enc_out.at[0, part, :], sems.at[3 + c])
        copy.start()
        copies.append(copy)
    for copy in copies:
        copy.wait()


def on_device(layer_acts, enc_weight, dec_weight, enc_bias, dec_bias, block_ids, block_counts):
    n_layer = lax.axis_size("layer")
    n_lat = lax.axis_size("latent")
    n_dp = lax.axis_size("dp")
    rows, width = layer_acts.shape[1:]
    lat = enc_weight.shape[2]
    tiles, blocks = block_ids.shape[1:]
    group_rows = rows * n_lat
    chips = n_lat // CORES
    splits = SPLITS if width % (128 * SPLITS) == 0 else 1
    half = width // n_dp
    any_spec = pl.BlockSpec(memory_space=pltpu.HBM)
    vmem_spec = pl.BlockSpec(memory_space=pltpu.VMEM)
    dma = lambda *shape: pltpu.SemaphoreType.DMA(shape)
    staged = pl.pallas_call(
        functools.partial(step_kernel, n_layer, n_lat, n_dp),
        out_shape=(
            pltpu.VMEM((half, n_dp * group_rows), BF16),
            pltpu.VMEM((n_dp * group_rows, lat), BF16),
            pltpu.VMEM((lat, half), BF16),
            pltpu.VMEM((lat // n_dp,), F32),
            pltpu.VMEM((1, half), F32),
        ),
        in_specs=[any_spec] * 7,
        out_specs=(vmem_spec,) * 5,
        scratch_shapes=[
            pltpu.VMEM((n_lat, rows, width), BF16),
            pltpu.VMEM((width, lat), BF16),
            pltpu.VMEM((lat, width), BF16),
            pltpu.VMEM((lat,), F32),
            pltpu.VMEM((1, width), F32),
            pltpu.VMEM((blocks, tiles), jnp.int32),
            pltpu.VMEM((1, tiles), jnp.int32),
            pltpu.VMEM((n_dp, n_lat, rows, half), BF16),
            pltpu.VMEM((group_rows, lat), BF16),
            pltpu.VMEM((n_layer, group_rows, lat), BF16),
            pltpu.VMEM((group_rows, lat), BF16),
            pltpu.VMEM((n_dp, group_rows, lat), BF16),
            pltpu.VMEM((CORES, chips, rows, width), BF16),
            pltpu.VMEM((chips, rows, width), BF16),
            pltpu.VMEM((chips, rows, width), BF16),
            pltpu.VMEM((chips, rows, width), BF16),
            pltpu.VMEM((n_lat, rows, width), BF16),
            pltpu.VMEM((n_dp, n_lat, rows, half), BF16),
            pltpu.VMEM((group_rows, lat), BF16),
            pltpu.VMEM((n_layer, n_dp, group_rows, lat), BF16),
            pltpu.VMEM((group_rows, lat), BF16),
            pltpu.VMEM((n_dp, group_rows, lat), BF16),
            dma(7),
            dma(2 * chips - 1, splits), dma(n_lat, splits),
            dma(n_dp - 1, n_lat), dma(n_dp, n_lat),
            dma(n_layer - 1), dma(n_layer),
            dma(n_dp - 1), dma(n_dp),
            dma(splits), dma(splits),
            dma(chips - 1, splits), dma(chips, splits),
            dma(2 * chips - 1, splits), dma(n_lat, splits),
            dma(n_dp - 1, n_lat), dma(n_dp, n_lat),
            dma(n_layer * n_dp - 1), dma(n_layer, n_dp),
            dma(n_dp - 1), dma(n_dp),
        ],
        compiler_params=pltpu.CompilerParams(
            collective_id=0, has_side_effects=True, vmem_limit_bytes=40 << 20
        ),
        name="crosscoder_step",
    )(*[
        pltpu.with_memory_space_constraint(x, pltpu.HBM)
        for x in (
            layer_acts, enc_weight, dec_weight, enc_bias, dec_bias,
            jnp.swapaxes(block_ids, 1, 2), block_counts,
        )
    ])
    return pl.pallas_call(
        finish_kernel,
        out_shape=(
            jax.ShapeDtypeStruct((1, half, lat), BF16),
            jax.ShapeDtypeStruct((1, lat, half), BF16),
            jax.ShapeDtypeStruct((lat // n_dp,), F32),
            jax.ShapeDtypeStruct((1, half), F32),
        ),
        in_specs=[vmem_spec] * 5,
        out_specs=(any_spec,) * 4,
        scratch_shapes=[pltpu.VMEM((half, lat), BF16), dma(3 + ENC_CHUNKS)],
        compiler_params=pltpu.CompilerParams(vmem_limit_bytes=16 << 20),
        name="crosscoder_finish",
    )(*staged)


def solution(mesh):
    in_specs = (
        P("layer", ("latent", "dp"), None),
        P("layer", None, "latent"),
        P("layer", "latent", None),
        P("latent"),
        P("layer", None),
        P("latent", None, None),
        P("latent", None),
    )
    out_specs = (
        P("layer", "dp", "latent"),
        P("layer", "latent", "dp"),
        P(("latent", "dp")),
        P("layer", "dp"),
    )
    return jax.shard_map(
        on_device, mesh=mesh, in_specs=in_specs, out_specs=out_specs, check_vma=False
    )
```

```python
import functools
import math

import jax
import jax.numpy as jnp
from jax import lax
from jax.experimental import pallas as pl
from jax.experimental.pallas import tpu as pltpu
from jax.sharding import PartitionSpec as P

SPARSITY = 0.5
NORM_EPS = 1e-06
MESH = pl.DeviceIdType.MESH
F32 = jnp.float32
BF16 = jnp.bfloat16
ENC_CHUNKS = 4
CORES = 2


def chip_peers_of(chip, chips):
    if chips & (chips - 1):
        return [lax.rem(chip + k, chips) for k in range(1, chips)]
    peers = []
    for k in sorted(range(1, chips), key=lambda k: (-bin(k).count("1"), -k)):
        peer = chip
        for b in range(chips.bit_length() - 1):
            if k >> b & 1:
                peer = peer + (1 << b) - (2 << b) * lax.rem(chip // (1 << b), 2)
        peers.append(peer)
    return peers


def step_kernel(
    n_layer, n_lat, n_dp,
    acts_hbm, enc_hbm, dec_hbm, ebias_hbm, dbias_hbm, ids_hbm, counts_hbm,
    acts_t, pg_out, dec_stage, eb_stage, db_stage,
    acts_all, enc_v, dec_v, ebias_v, dbias_v, ids_v, counts_v,
    dec_t, acts_half, pre_send, pre_recv, codes_send, codes_recv,
    part_send, pair_recv, chip_send, part_recv, err_all, err_half, grad_send, grad_recv,
    gate_send, gate_recv,
    in_sems, acts_ss, acts_rs, ahalf_ss, ahalf_rs, pre_ss, pre_rs, codes_ss, codes_rs,
    pair_ss, pair_rs, part_ss, part_rs, err_ss, err_rs, ehalf_ss, ehalf_rs, grad_ss, grad_rs, gate_ss, gate_rs,
):
    layer = lax.axis_index("layer")
    me = lax.axis_index("latent")
    group = lax.axis_index("dp")
    rows = acts_all.shape[1]
    width = acts_all.shape[2]
    lat = enc_v.shape[1]
    blocks, tiles = ids_v.shape
    rows_group = rows * n_lat
    half = width // n_dp
    lat_part = lat // n_dp
    scale = 1.0 / math.sqrt(rows_group * n_dp)

    chips = n_lat // CORES
    chip = me // CORES
    core = lax.rem(me, CORES)
    partner = chip * CORES + 1 - core
    chip_peers = chip_peers_of(chip, chips)
    n_peers = len(chip_peers)
    lat_peers = [lax.rem(me + k, n_lat) for k in range(1, n_lat)]
    layer_peers = [lax.rem(layer + k, n_layer) for k in range(1, n_layer)]
    dp_peers = [lax.rem(group + k, n_dp) for k in range(1, n_dp)]
    n_z = n_layer * n_dp
    rank = layer * n_dp + group
    others = [i + lax.div(i - rank + n_z, n_z) for i in range(n_z - 1)]
    z_peers = [(lax.div(i, n_dp), lax.rem(i, n_dp)) for i in others]

    own_acts = pltpu.make_async_copy(acts_hbm.at[0], acts_all.at[me], in_sems.at[0])
    own_acts.start()
    loads = [
        pltpu.make_async_copy(src, dst, in_sems.at[i + 1])
        for i, (src, dst) in enumerate(
            (
                (enc_hbm.at[0], enc_v),
                (dec_hbm.at[0], dec_v),
                (ebias_hbm, ebias_v),
                (dbias_hbm, dbias_v),
                (ids_hbm.at[0], ids_v),
                (counts_hbm, counts_v),
            )
        )
    ]
    for load in loads:
        load.start()

    barrier = pltpu.get_barrier_semaphore()
    for p in lat_peers:
        pl.semaphore_signal(barrier, inc=1, device_id={"latent": p}, device_id_type=MESH)
    for p, d in z_peers:
        pl.semaphore_signal(barrier, inc=1, device_id={"layer": p, "dp": d}, device_id_type=MESH)
    with jax.named_scope("entry"):
        pl.semaphore_wait(barrier, len(lat_peers) + len(z_peers))

    def remote(src, dst, ss, rs, axis, peer):
        return pltpu.make_async_remote_copy(
            src_ref=src, dst_ref=dst, send_sem=ss, recv_sem=rs,
            device_id={axis: peer}, device_id_type=MESH,
        )

    sent = []

    def send(*args):
        copy = remote(*args)
        copy.start()
        sent.append(copy)

    def share(buf, ss, rs):
        mine = buf.at[me]
        targets = [q * CORES + 1 - core for q in chip_peers] + [partner]
        for k, j in enumerate(targets):
            send(mine, mine, ss.at[k], rs.at[me], "latent", j)

    def wait_block(buf, ss, rs, j):
        remote(buf.at[j], buf.at[j], ss.at[0], rs.at[j], "latent", partner).wait_recv()

    def gather(buf, ss, rs, beside):
        for k, q in enumerate(chip_peers):
            j = q * CORES + 1 - core
            with jax.named_scope("relay"):
                wait_block(buf, ss, rs, j)
            send(buf.at[j], buf.at[j], ss.at[n_peers + 1 + k], rs.at[j], "latent", partner)
        beside()
        with jax.named_scope("direct"):
            for j in [partner]:
                wait_block(buf, ss, rs, j)
        with jax.named_scope("relayed"):
            for q in chip_peers:
                wait_block(buf, ss, rs, q * CORES + core)
        return buf[...].astype(F32).reshape(rows_group, width).astype(BF16)

    def cross(src, dst_half, ss, rs):
        for q, p in enumerate(dp_peers):
            cols = pl.ds(pl.multiple_of(p * half, 128), half)
            send(src.at[:, cols], dst_half.at[group, me], ss.at[q, 0], rs.at[group, me], "dp", p)

    own_acts.wait()
    share(acts_all, acts_ss, acts_rs)
    cross(acts_all.at[me], acts_half, ahalf_ss, ahalf_rs)

    for load in loads:
        load.wait()
    dec_f = dec_v[...].astype(F32)
    norm_col = jnp.sqrt(jnp.sum(dec_f * dec_f, axis=1, keepdims=True) + NORM_EPS)
    r_i = lax.broadcasted_iota(jnp.int32, (lat, lat), 0)
    c_i = lax.broadcasted_iota(jnp.int32, (lat, lat), 1)
    norm_row = jnp.sum(
        jnp.where(r_i == c_i, jnp.broadcast_to(norm_col, (lat, lat)), 0.0), axis=0, keepdims=True
    )
    dec_t[...] = dec_v[...].T
    ids_i = ids_v[...]
    counts_i = counts_v[...]
    lat_block = lax.broadcasted_iota(jnp.int32, (rows_group, lat), 1) // (lat // blocks)
    pick_r = lax.broadcasted_iota(jnp.int32, (rows_group, tiles), 0) // rows
    pick_c = lax.broadcasted_iota(jnp.int32, (rows_group, tiles), 1)
    picked = pick_c == pick_r * n_dp + group
    mask = jnp.zeros((rows_group, lat), F32)
    for b in range(blocks):
        hit = jnp.zeros((1, tiles), F32)
        for k in range(blocks):
            hit = jnp.where((ids_i[k : k + 1, :] == b) & (counts_i > k), 1.0, hit)
        row_hit = jnp.sum(
            jnp.where(picked, jnp.broadcast_to(hit, (rows_group, tiles)), 0.0), axis=1, keepdims=True
        )
        mask = jnp.where(lat_block == b, jnp.broadcast_to(row_hit, (rows_group, lat)), mask)

    def wait_half(dst_half, ss, rs, p, j):
        remote(
            dst_half.at[p, j], dst_half.at[p, j], ss.at[0, 0], rs.at[p, j], "latent", lat_peers[0]
        ).wait_recv()

    def spread(dst_half, ss, rs):
        for q, p in enumerate(dp_peers):
            with jax.named_scope("half"):
                wait_half(dst_half, ss, rs, p, me)
            for k, j in enumerate(lat_peers):
                send(dst_half.at[p, me], dst_half.at[p, me], ss.at[q, k + 1], rs.at[p, me], "latent", j)

    gathered = gather(acts_all, acts_ss, acts_rs, lambda: None)
    pre = jnp.dot(gathered, enc_v[...], preferred_element_type=F32)
    pre_send[...] = pre.astype(BF16)
    for k, p in enumerate(layer_peers):
        send(pre_send, pre_recv.at[layer], pre_ss.at[k], pre_rs.at[layer], "layer", p)
    spread(acts_half, ahalf_ss, ahalf_rs)
    pre = pre + ebias_v[...][None, :]
    for k, p in enumerate(layer_peers):
        with jax.named_scope("layers"):
            remote(pre_send, pre_recv.at[p], pre_ss.at[k], pre_rs.at[p], "layer", p).wait_recv()
        pre = pre + pre_recv[p].astype(F32)

    codes = (jax.nn.softplus(pre) * mask).astype(BF16)
    codes_send[...] = codes
    part = jnp.dot(codes, dec_v[...], preferred_element_type=F32)
    part_send[...] = part.reshape(n_lat, rows, width).astype(BF16)
    for k, q in enumerate(chip_peers):
        send(
            part_send.at[q * CORES + core], pair_recv.at[k],
            pair_ss.at[k], pair_rs.at[k], "latent", partner,
        )
    for k, j in enumerate([partner]):
        send(part_send.at[j], part_recv.at[me], part_ss.at[n_peers + k], part_rs.at[me], "latent", j)
    for k, q in enumerate(chip_peers):
        with jax.named_scope("pair"):
            remote(
                pair_recv.at[k], pair_recv.at[k], pair_ss.at[k], pair_rs.at[k], "latent", partner
            ).wait_recv()
        total = part_send[q * CORES + 1 - core].astype(F32) + pair_recv[k].astype(F32)
        chip_send[k] = total.astype(BF16)
        send(
            chip_send.at[k], part_recv.at[me], part_ss.at[k], part_rs.at[me],
            "latent", q * CORES + 1 - core,
        )
    for k, p in enumerate(dp_peers):
        send(codes_send, codes_recv.at[group], codes_ss.at[k], codes_rs.at[group], "dp", p)

    mine_cols = pl.ds(pl.multiple_of(group * half, 128), half)
    acts_rows = [acts_all[:, :, mine_cols].astype(F32).reshape(rows_group, half)]
    for q, p in enumerate(dp_peers):
        with jax.named_scope("halves"):
          for j in lat_peers:
            wait_half(acts_half, ahalf_ss, ahalf_rs, p, j)
        acts_rows.append(acts_half[p].astype(F32).reshape(rows_group, half))
    acts_t[...] = jnp.concatenate(acts_rows, axis=0).T.astype(BF16)

    gate = mask * jax.nn.sigmoid(pre)
    gate_send[...] = gate.astype(BF16)
    for k, p in enumerate(dp_peers):
        send(gate_send, gate_recv.at[group], gate_ss.at[k], gate_rs.at[group], "dp", p)

    recon = part_send[me].astype(F32) + dbias_v[...]
    for j in [partner] + [q * CORES + 1 - core for q in chip_peers]:
        with jax.named_scope("chips"):
            wait_block(part_recv, part_ss, part_rs, j)
        recon = recon + part_recv[j].astype(F32)
    err_all[me] = (scale * (recon - acts_all[me].astype(F32))).astype(BF16)
    share(err_all, err_ss, err_rs)
    cross(err_all.at[me], err_half, ehalf_ss, ehalf_rs)

    code_rows = [codes.astype(F32)]
    for k, p in enumerate(dp_peers):
        remote(codes_send, codes_recv.at[p], codes_ss.at[k], codes_rs.at[p], "dp", p).wait_recv()
        code_rows.append(codes_recv[p].astype(F32))
    codes_t = jnp.concatenate(code_rows, axis=0).T
    totals = jnp.sum(codes_t, axis=1, keepdims=True)
    unit_gain = SPARSITY * scale * totals / norm_col
    codes_t = codes_t.astype(BF16)

    err = gather(err_all, err_ss, err_rs, lambda: spread(err_half, ehalf_ss, ehalf_rs))
    grad = jnp.dot(err, dec_t[...], preferred_element_type=F32)
    grad = grad + SPARSITY * scale * norm_row
    grad_send[...] = grad.astype(BF16)
    for k, (p, d) in enumerate(z_peers):
        copy = pltpu.make_async_remote_copy(
            src_ref=grad_send, dst_ref=grad_recv.at[layer, group],
            send_sem=grad_ss.at[k], recv_sem=grad_rs.at[layer, group],
            device_id={"layer": p, "dp": d}, device_id_type=MESH,
        )
        copy.start()
        sent.append(copy)

    err_rows = [err_all[:, :, mine_cols].astype(F32).reshape(rows_group, half)]
    for q, p in enumerate(dp_peers):
        with jax.named_scope("halves"):
          for j in lat_peers:
            wait_half(err_half, ehalf_ss, ehalf_rs, p, j)
        err_rows.append(err_half[p].astype(F32).reshape(rows_group, half))
    err_rows = jnp.concatenate(err_rows, axis=0)
    db_stage[...] = jnp.sum(err_rows, axis=0, keepdims=True)
    dec_grad = jnp.dot(codes_t, err_rows.astype(BF16), preferred_element_type=F32)
    dec_grad = dec_grad + unit_gain * dec_v[:, mine_cols].astype(F32)
    dec_stage[...] = dec_grad.astype(BF16)

    gates = [gate]
    for k, d in enumerate(dp_peers):
        remote(gate_send, gate_recv.at[d], gate_ss.at[k], gate_rs.at[d], "dp", d).wait_recv()
        gates.append(gate_recv[d].astype(F32))

    def wait_grad(p, d):
        with jax.named_scope("zgrad"):
          remote(grad_send, grad_recv.at[p, d], grad_ss.at[0], grad_rs.at[p, d], "latent", partner).wait_recv()
        return grad_recv[p, d].astype(F32)

    for p in layer_peers:
        grad = grad + wait_grad(p, group)
    pg_rows = [(grad * gates[0]).astype(BF16)]
    for k, d in enumerate(dp_peers):
        other = wait_grad(layer, d)
        for p in layer_peers:
            other = other + wait_grad(p, d)
        pg_rows.append((other * gates[k + 1]).astype(BF16))
    pg_rows = jnp.concatenate(pg_rows, axis=0)
    pg_out[...] = pg_rows
    bias_sum = jnp.sum(pg_rows.astype(F32), axis=0, keepdims=True)
    bias_mine = bias_sum[:, :lat_part]
    for d in range(1, n_dp):
        bias_mine = jnp.where(group == d, bias_sum[:, d * lat_part : (d + 1) * lat_part], bias_mine)
    eb_stage[...] = bias_mine.reshape(lat_part)
    with jax.named_scope("sends"):
      for copy in sent:
        copy.wait_send()


def finish_kernel(
    acts_t, pg_rows, dec_grad, eb_grad, db_grad, enc_out, dec_out, eb_out, db_out, enc_stage, sems
):
    copies = [
        pltpu.make_async_copy(dec_grad, dec_out.at[0], sems.at[0]),
        pltpu.make_async_copy(eb_grad, eb_out, sems.at[1]),
        pltpu.make_async_copy(db_grad, db_out, sems.at[2]),
    ]
    for copy in copies:
        copy.start()
    size = acts_t.shape[0] // ENC_CHUNKS
    for c in range(ENC_CHUNKS):
        part = pl.ds(c * size, size)
        enc_stage[part, :] = jnp.dot(
            acts_t[part, :], pg_rows[...], preferred_element_type=F32
        ).astype(BF16)
        copy = pltpu.make_async_copy(enc_stage.at[part, :], enc_out.at[0, part, :], sems.at[3 + c])
        copy.start()
        copies.append(copy)
    for copy in copies:
        copy.wait()


def on_device(layer_acts, enc_weight, dec_weight, enc_bias, dec_bias, block_ids, block_counts):
    n_layer = lax.axis_size("layer")
    n_lat = lax.axis_size("latent")
    n_dp = lax.axis_size("dp")
    rows, width = layer_acts.shape[1:]
    lat = enc_weight.shape[2]
    tiles, blocks = block_ids.shape[1:]
    group_rows = rows * n_lat
    chips = n_lat // CORES
    half = width // n_dp
    any_spec = pl.BlockSpec(memory_space=pltpu.HBM)
    vmem_spec = pl.BlockSpec(memory_space=pltpu.VMEM)
    dma = lambda *shape: pltpu.SemaphoreType.DMA(shape)
    staged = pl.pallas_call(
        functools.partial(step_kernel, n_layer, n_lat, n_dp),
        out_shape=(
            pltpu.VMEM((half, n_dp * group_rows), BF16),
            pltpu.VMEM((n_dp * group_rows, lat), BF16),
            pltpu.VMEM((lat, half), BF16),
            pltpu.VMEM((lat // n_dp,), F32),
            pltpu.VMEM((1, half), F32),
        ),
        in_specs=[any_spec] * 7,
        out_specs=(vmem_spec,) * 5,
        scratch_shapes=[
            pltpu.VMEM((n_lat, rows, width), BF16),
            pltpu.VMEM((width, lat), BF16),
            pltpu.VMEM((lat, width), BF16),
            pltpu.VMEM((lat,), F32),
            pltpu.VMEM((1, width), F32),
            pltpu.VMEM((blocks, tiles), jnp.int32),
            pltpu.VMEM((1, tiles), jnp.int32),
            pltpu.VMEM((width, lat), BF16),
            pltpu.VMEM((n_dp, n_lat, rows, half), BF16),
            pltpu.VMEM((group_rows, lat), BF16),
            pltpu.VMEM((n_layer, group_rows, lat), BF16),
            pltpu.VMEM((group_rows, lat), BF16),
            pltpu.VMEM((n_dp, group_rows, lat), BF16),
            pltpu.VMEM((n_lat, rows, width), BF16),
            pltpu.VMEM((chips, rows, width), BF16),
            pltpu.VMEM((chips, rows, width), BF16),
            pltpu.VMEM((n_lat, rows, width), BF16),
            pltpu.VMEM((n_lat, rows, width), BF16),
            pltpu.VMEM((n_dp, n_lat, rows, half), BF16),
            pltpu.VMEM((group_rows, lat), BF16),
            pltpu.VMEM((n_layer, n_dp, group_rows, lat), BF16),
            pltpu.VMEM((group_rows, lat), BF16),
            pltpu.VMEM((n_dp, group_rows, lat), BF16),
            dma(7),
            dma(2 * chips - 1), dma(n_lat),
            dma(n_dp - 1, n_lat), dma(n_dp, n_lat),
            dma(n_layer - 1), dma(n_layer),
            dma(n_dp - 1), dma(n_dp),
            dma(chips), dma(chips),
            dma(n_lat), dma(n_lat),
            dma(2 * chips - 1), dma(n_lat),
            dma(n_dp - 1, n_lat), dma(n_dp, n_lat),
            dma(n_layer * n_dp - 1), dma(n_layer, n_dp),
            dma(n_dp - 1), dma(n_dp),
        ],
        compiler_params=pltpu.CompilerParams(
            collective_id=0, has_side_effects=True, vmem_limit_bytes=40 << 20
        ),
        name="crosscoder_step",
    )(*[
        pltpu.with_memory_space_constraint(x, pltpu.HBM)
        for x in (
            layer_acts, enc_weight, dec_weight, enc_bias, dec_bias,
            jnp.swapaxes(block_ids, 1, 2), block_counts,
        )
    ])
    return pl.pallas_call(
        finish_kernel,
        out_shape=(
            jax.ShapeDtypeStruct((1, half, lat), BF16),
            jax.ShapeDtypeStruct((1, lat, half), BF16),
            jax.ShapeDtypeStruct((lat // n_dp,), F32),
            jax.ShapeDtypeStruct((1, half), F32),
        ),
        in_specs=[vmem_spec] * 5,
        out_specs=(any_spec,) * 4,
        scratch_shapes=[pltpu.VMEM((half, lat), BF16), dma(3 + ENC_CHUNKS)],
        compiler_params=pltpu.CompilerParams(vmem_limit_bytes=16 << 20),
        name="crosscoder_finish",
    )(*staged)


def solution(mesh):
    in_specs = (
        P("layer", ("latent", "dp"), None),
        P("layer", None, "latent"),
        P("layer", "latent", None),
        P("latent"),
        P("layer", None),
        P("latent", None, None),
        P("latent", None),
    )
    out_specs = (
        P("layer", "dp", "latent"),
        P("layer", "latent", "dp"),
        P(("latent", "dp")),
        P("layer", "dp"),
    )
    return jax.shard_map(
        on_device, mesh=mesh, in_specs=in_specs, out_specs=out_specs, check_vma=False
    )
```

```python
import functools
import math

import jax
import jax.numpy as jnp
from jax import lax
from jax.experimental import pallas as pl
from jax.experimental.pallas import tpu as pltpu
from jax.sharding import PartitionSpec as P

SPARSITY = 0.5
NORM_EPS = 1e-06
MESH = pl.DeviceIdType.MESH
F32 = jnp.float32
BF16 = jnp.bfloat16
ENC_CHUNKS = 4
CORES = 2


def chip_peers_of(chip, chips):
    if chips & (chips - 1):
        return [lax.rem(chip + k, chips) for k in range(1, chips)]
    peers = []
    for k in sorted(range(1, chips), key=lambda k: (-bin(k).count("1"), -k)):
        peer = chip
        for b in range(chips.bit_length() - 1):
            if k >> b & 1:
                peer = peer + (1 << b) - (2 << b) * lax.rem(chip // (1 << b), 2)
        peers.append(peer)
    return peers


def step_kernel(
    n_layer, n_lat, n_dp,
    acts_hbm, enc_hbm, dec_hbm, ebias_hbm, dbias_hbm, ids_hbm, counts_hbm,
    acts_t, pg_out, dec_stage, eb_stage, db_stage,
    acts_all, enc_v, dec_v, ebias_v, dbias_v, ids_v, counts_v,
    dec_t, acts_half, pre_send, pre_recv, codes_send, codes_recv,
    part_send, pair_recv, chip_send, part_recv, err_all, err_half, grad_send, grad_recv,
    gate_send, gate_recv,
    in_sems, send_sem, acts_rs, ahalf_rs, pre_rs, codes_rs,
    pair_rs, part_rs, err_rs, ehalf_rs, grad_rs, gate_rs,
):
    layer = lax.axis_index("layer")
    me = lax.axis_index("latent")
    group = lax.axis_index("dp")
    rows = acts_all.shape[1]
    width = acts_all.shape[2]
    lat = enc_v.shape[1]
    blocks, tiles = ids_v.shape
    rows_group = rows * n_lat
    half = width // n_dp
    lat_part = lat // n_dp
    scale = 1.0 / math.sqrt(rows_group * n_dp)

    chips = n_lat // CORES
    chip = me // CORES
    core = lax.rem(me, CORES)
    partner = chip * CORES + 1 - core
    chip_peers = chip_peers_of(chip, chips)
    n_peers = len(chip_peers)
    lat_peers = [lax.rem(me + k, n_lat) for k in range(1, n_lat)]
    layer_peers = [lax.rem(layer + k, n_layer) for k in range(1, n_layer)]
    dp_peers = [lax.rem(group + k, n_dp) for k in range(1, n_dp)]
    n_z = n_layer * n_dp
    rank = layer * n_dp + group
    others = [i + lax.div(i - rank + n_z, n_z) for i in range(n_z - 1)]
    z_peers = [(lax.div(i, n_dp), lax.rem(i, n_dp)) for i in others]

    own_acts = pltpu.make_async_copy(acts_hbm.at[0], acts_all.at[me], in_sems.at[0])
    own_acts.start()
    loads = [
        pltpu.make_async_copy(src, dst, in_sems.at[i + 1])
        for i, (src, dst) in enumerate(
            (
                (enc_hbm.at[0], enc_v),
                (dec_hbm.at[0], dec_v),
                (ebias_hbm, ebias_v),
                (dbias_hbm, dbias_v),
                (ids_hbm.at[0], ids_v),
                (counts_hbm, counts_v),
            )
        )
    ]
    for load in loads:
        load.start()

    barrier = pltpu.get_barrier_semaphore()
    for p in lat_peers:
        pl.semaphore_signal(barrier, inc=1, device_id={"latent": p}, device_id_type=MESH)
    for p in layer_peers:
        pl.semaphore_signal(barrier, inc=1, device_id={"layer": p}, device_id_type=MESH)
    for p in dp_peers:
        pl.semaphore_signal(barrier, inc=1, device_id={"dp": p}, device_id_type=MESH)
    with jax.named_scope("entry"):
        pl.semaphore_wait(barrier, n_lat + n_layer + n_dp - 3)

    def remote(src, dst, rs, axis, peer):
        return pltpu.make_async_remote_copy(
            src_ref=src, dst_ref=dst, send_sem=send_sem.at[0], recv_sem=rs,
            device_id={axis: peer}, device_id_type=MESH,
        )

    sent = []

    def send(*args):
        copy = remote(*args)
        copy.start()
        sent.append(copy)

    def share(buf, rs):
        mine = buf.at[me]
        targets = [q * CORES + 1 - core for q in chip_peers] + [partner]
        for k, j in enumerate(targets):
            send(mine, mine, rs.at[me], "latent", j)

    def wait_block(buf, rs, j):
        remote(buf.at[j], buf.at[j], rs.at[j], "latent", partner).wait_recv()

    def gather(buf, rs, beside):
        for k, q in enumerate(chip_peers):
            j = q * CORES + 1 - core
            with jax.named_scope("relay"):
                wait_block(buf, rs, j)
            send(buf.at[j], buf.at[j], rs.at[j], "latent", partner)
        beside()
        with jax.named_scope("direct"):
            for j in [partner]:
                wait_block(buf, rs, j)
        with jax.named_scope("relayed"):
            for q in chip_peers:
                wait_block(buf, rs, q * CORES + core)
        return buf[...].astype(F32).reshape(rows_group, width).astype(BF16)

    def cross(src, dst_half, rs):
        for q, p in enumerate(dp_peers):
            cols = pl.ds(pl.multiple_of(p * half, 128), half)
            send(src.at[:, cols], dst_half.at[group, me], rs.at[group, me], "dp", p)

    own_acts.wait()
    share(acts_all, acts_rs)
    cross(acts_all.at[me], acts_half, ahalf_rs)

    for load in loads:
        load.wait()
    dec_f = dec_v[...].astype(F32)
    norm_col = jnp.sqrt(jnp.sum(dec_f * dec_f, axis=1, keepdims=True) + NORM_EPS)
    r_i = lax.broadcasted_iota(jnp.int32, (lat, lat), 0)
    c_i = lax.broadcasted_iota(jnp.int32, (lat, lat), 1)
    norm_row = jnp.sum(
        jnp.where(r_i == c_i, jnp.broadcast_to(norm_col, (lat, lat)), 0.0), axis=0, keepdims=True
    )
    dec_t[...] = dec_v[...].T
    ids_i = ids_v[...]
    counts_i = counts_v[...]
    lat_block = lax.broadcasted_iota(jnp.int32, (rows_group, lat), 1) // (lat // blocks)
    pick_r = lax.broadcasted_iota(jnp.int32, (rows_group, tiles), 0) // rows
    pick_c = lax.broadcasted_iota(jnp.int32, (rows_group, tiles), 1)
    picked = pick_c == pick_r * n_dp + group
    mask = jnp.zeros((rows_group, lat), F32)
    for b in range(blocks):
        hit = jnp.zeros((1, tiles), F32)
        for k in range(blocks):
            hit = jnp.where((ids_i[k : k + 1, :] == b) & (counts_i > k), 1.0, hit)
        row_hit = jnp.sum(
            jnp.where(picked, jnp.broadcast_to(hit, (rows_group, tiles)), 0.0), axis=1, keepdims=True
        )
        mask = jnp.where(lat_block == b, jnp.broadcast_to(row_hit, (rows_group, lat)), mask)

    def wait_half(dst_half, rs, p, j):
        remote(
            dst_half.at[p, j], dst_half.at[p, j], rs.at[p, j], "latent", lat_peers[0]
        ).wait_recv()

    def spread(dst_half, rs):
        for q, p in enumerate(dp_peers):
            with jax.named_scope("half"):
                wait_half(dst_half, rs, p, me)
            for k, j in enumerate(lat_peers):
                send(dst_half.at[p, me], dst_half.at[p, me], rs.at[p, me], "latent", j)

    gathered = gather(acts_all, acts_rs, lambda: None)
    pre = jnp.dot(gathered, enc_v[...], preferred_element_type=F32)
    pre_send[...] = pre.astype(BF16)
    for k, p in enumerate(layer_peers):
        send(pre_send, pre_recv.at[layer], pre_rs.at[layer], "layer", p)
    spread(acts_half, ahalf_rs)
    pre = pre + ebias_v[...][None, :]
    for k, p in enumerate(layer_peers):
        with jax.named_scope("layers"):
            remote(pre_send, pre_recv.at[p], pre_rs.at[p], "layer", p).wait_recv()
        pre = pre + pre_recv[p].astype(F32)

    codes = (jax.nn.softplus(pre) * mask).astype(BF16)
    codes_send[...] = codes
    part = jnp.dot(codes, dec_v[...], preferred_element_type=F32)
    part_send[...] = part.reshape(n_lat, rows, width).astype(BF16)
    for k, q in enumerate(chip_peers):
        send(
            part_send.at[q * CORES + core], pair_recv.at[k],
            pair_rs.at[k], "latent", partner,
        )
    for k, j in enumerate([partner]):
        send(part_send.at[j], part_recv.at[me], part_rs.at[me], "latent", j)
    for k, q in enumerate(chip_peers):
        with jax.named_scope("pair"):
            remote(
                pair_recv.at[k], pair_recv.at[k], pair_rs.at[k], "latent", partner
            ).wait_recv()
        total = part_send[q * CORES + 1 - core].astype(F32) + pair_recv[k].astype(F32)
        chip_send[k] = total.astype(BF16)
        send(
            chip_send.at[k], part_recv.at[me], part_rs.at[me],
            "latent", q * CORES + 1 - core,
        )
    for k, p in enumerate(dp_peers):
        send(codes_send, codes_recv.at[group], codes_rs.at[group], "dp", p)

    mine_cols = pl.ds(pl.multiple_of(group * half, 128), half)
    acts_rows = [acts_all[:, :, mine_cols].astype(F32).reshape(rows_group, half)]
    for q, p in enumerate(dp_peers):
        with jax.named_scope("halves"):
          for j in lat_peers:
            wait_half(acts_half, ahalf_rs, p, j)
        acts_rows.append(acts_half[p].astype(F32).reshape(rows_group, half))
    acts_t[...] = jnp.concatenate(acts_rows, axis=0).T.astype(BF16)

    gate = mask * jax.nn.sigmoid(pre)
    gate_send[...] = gate.astype(BF16)
    for k, p in enumerate(dp_peers):
        send(gate_send, gate_recv.at[group], gate_rs.at[group], "dp", p)

    recon = part_send[me].astype(F32) + dbias_v[...]
    for j in [partner] + [q * CORES + 1 - core for q in chip_peers]:
        with jax.named_scope("chips"):
            wait_block(part_recv, part_rs, j)
        recon = recon + part_recv[j].astype(F32)
    err_all[me] = (scale * (recon - acts_all[me].astype(F32))).astype(BF16)
    share(err_all, err_rs)
    cross(err_all.at[me], err_half, ehalf_rs)

    code_rows = [codes.astype(F32)]
    for k, p in enumerate(dp_peers):
        remote(codes_send, codes_recv.at[p], codes_rs.at[p], "dp", p).wait_recv()
        code_rows.append(codes_recv[p].astype(F32))
    codes_t = jnp.concatenate(code_rows, axis=0).T
    totals = jnp.sum(codes_t, axis=1, keepdims=True)
    unit_gain = SPARSITY * scale * totals / norm_col
    codes_t = codes_t.astype(BF16)

    err = gather(err_all, err_rs, lambda: spread(err_half, ehalf_rs))
    grad = jnp.dot(err, dec_t[...], preferred_element_type=F32)
    grad = grad + SPARSITY * scale * norm_row
    grad_send[...] = grad.astype(BF16)
    gates = [gate]
    for k, d in enumerate(dp_peers):
        remote(gate_send, gate_recv.at[d], gate_rs.at[d], "dp", d).wait_recv()
        gates.append(gate_recv[d].astype(F32))
    for k, (p, d) in enumerate(z_peers):
        copy = pltpu.make_async_remote_copy(
            src_ref=grad_send, dst_ref=grad_recv.at[layer, group],
            send_sem=send_sem.at[0], recv_sem=grad_rs.at[layer, group],
            device_id={"layer": p, "dp": d}, device_id_type=MESH,
        )
        copy.start()
        sent.append(copy)

    err_rows = [err_all[:, :, mine_cols].astype(F32).reshape(rows_group, half)]
    for q, p in enumerate(dp_peers):
        with jax.named_scope("halves"):
          for j in lat_peers:
            wait_half(err_half, ehalf_rs, p, j)
        err_rows.append(err_half[p].astype(F32).reshape(rows_group, half))
    err_rows = jnp.concatenate(err_rows, axis=0)
    db_stage[...] = jnp.sum(err_rows, axis=0, keepdims=True)
    dec_grad = jnp.dot(codes_t, err_rows.astype(BF16), preferred_element_type=F32)
    dec_grad = dec_grad + unit_gain * dec_v[:, mine_cols].astype(F32)
    dec_stage[...] = dec_grad.astype(BF16)

    def wait_grad(p, d):
        with jax.named_scope("zgrad"):
          remote(grad_send, grad_recv.at[p, d], grad_rs.at[p, d], "latent", partner).wait_recv()
        return grad_recv[p, d].astype(F32)

    for p in layer_peers:
        grad = grad + wait_grad(p, group)
    pg_rows = [(grad * gates[0]).astype(BF16)]
    for k, d in enumerate(dp_peers):
        other = wait_grad(layer, d)
        for p in layer_peers:
            other = other + wait_grad(p, d)
        pg_rows.append((other * gates[k + 1]).astype(BF16))
    pg_rows = jnp.concatenate(pg_rows, axis=0)
    pg_out[...] = pg_rows
    bias_sum = jnp.sum(pg_rows.astype(F32), axis=0, keepdims=True)
    bias_mine = bias_sum[:, :lat_part]
    for d in range(1, n_dp):
        bias_mine = jnp.where(group == d, bias_sum[:, d * lat_part : (d + 1) * lat_part], bias_mine)
    eb_stage[...] = bias_mine.reshape(lat_part)
    with jax.named_scope("sends"):
      for copy in sent:
        copy.wait_send()


def finish_kernel(
    acts_t, pg_rows, dec_grad, eb_grad, db_grad, enc_out, dec_out, eb_out, db_out, enc_stage, sems
):
    copies = [
        pltpu.make_async_copy(dec_grad, dec_out.at[0], sems.at[0]),
        pltpu.make_async_copy(eb_grad, eb_out, sems.at[1]),
        pltpu.make_async_copy(db_grad, db_out, sems.at[2]),
    ]
    for copy in copies:
        copy.start()
    size = acts_t.shape[0] // ENC_CHUNKS
    for c in range(ENC_CHUNKS):
        part = pl.ds(c * size, size)
        enc_stage[part, :] = jnp.dot(
            acts_t[part, :], pg_rows[...], preferred_element_type=F32
        ).astype(BF16)
        copy = pltpu.make_async_copy(enc_stage.at[part, :], enc_out.at[0, part, :], sems.at[3 + c])
        copy.start()
        copies.append(copy)
    for copy in copies:
        copy.wait()


def on_device(layer_acts, enc_weight, dec_weight, enc_bias, dec_bias, block_ids, block_counts):
    n_layer = lax.axis_size("layer")
    n_lat = lax.axis_size("latent")
    n_dp = lax.axis_size("dp")
    rows, width = layer_acts.shape[1:]
    lat = enc_weight.shape[2]
    tiles, blocks = block_ids.shape[1:]
    group_rows = rows * n_lat
    chips = n_lat // CORES
    half = width // n_dp
    any_spec = pl.BlockSpec(memory_space=pltpu.HBM)
    vmem_spec = pl.BlockSpec(memory_space=pltpu.VMEM)
    dma = lambda *shape: pltpu.SemaphoreType.DMA(shape)
    staged = pl.pallas_call(
        functools.partial(step_kernel, n_layer, n_lat, n_dp),
        out_shape=(
            pltpu.VMEM((half, n_dp * group_rows), BF16),
            pltpu.VMEM((n_dp * group_rows, lat), BF16),
            pltpu.VMEM((lat, half), BF16),
            pltpu.VMEM((lat // n_dp,), F32),
            pltpu.VMEM((1, half), F32),
        ),
        in_specs=[any_spec] * 7,
        out_specs=(vmem_spec,) * 5,
        scratch_shapes=[
            pltpu.VMEM((n_lat, rows, width), BF16),
            pltpu.VMEM((width, lat), BF16),
            pltpu.VMEM((lat, width), BF16),
            pltpu.VMEM((lat,), F32),
            pltpu.VMEM((1, width), F32),
            pltpu.VMEM((blocks, tiles), jnp.int32),
            pltpu.VMEM((1, tiles), jnp.int32),
            pltpu.VMEM((width, lat), BF16),
            pltpu.VMEM((n_dp, n_lat, rows, half), BF16),
            pltpu.VMEM((group_rows, lat), BF16),
            pltpu.VMEM((n_layer, group_rows, lat), BF16),
            pltpu.VMEM((group_rows, lat), BF16),
            pltpu.VMEM((n_dp, group_rows, lat), BF16),
            pltpu.VMEM((n_lat, rows, width), BF16),
            pltpu.VMEM((chips, rows, width), BF16),
            pltpu.VMEM((chips, rows, width), BF16),
            pltpu.VMEM((n_lat, rows, width), BF16),
            pltpu.VMEM((n_lat, rows, width), BF16),
            pltpu.VMEM((n_dp, n_lat, rows, half), BF16),
            pltpu.VMEM((group_rows, lat), BF16),
            pltpu.VMEM((n_layer, n_dp, group_rows, lat), BF16),
            pltpu.VMEM((group_rows, lat), BF16),
            pltpu.VMEM((n_dp, group_rows, lat), BF16),
            dma(7), dma(1),
            dma(n_lat), dma(n_dp, n_lat), dma(n_layer), dma(n_dp),
            dma(chips), dma(n_lat), dma(n_lat), dma(n_dp, n_lat),
            dma(n_layer, n_dp), dma(n_dp),
        ],
        compiler_params=pltpu.CompilerParams(
            collective_id=0, has_side_effects=True, vmem_limit_bytes=40 << 20
        ),
        name="crosscoder_step",
    )(*[
        pltpu.with_memory_space_constraint(x, pltpu.HBM)
        for x in (
            layer_acts, enc_weight, dec_weight, enc_bias, dec_bias,
            jnp.swapaxes(block_ids, 1, 2), block_counts,
        )
    ])
    return pl.pallas_call(
        finish_kernel,
        out_shape=(
            jax.ShapeDtypeStruct((1, half, lat), BF16),
            jax.ShapeDtypeStruct((1, lat, half), BF16),
            jax.ShapeDtypeStruct((lat // n_dp,), F32),
            jax.ShapeDtypeStruct((1, half), F32),
        ),
        in_specs=[vmem_spec] * 5,
        out_specs=(any_spec,) * 4,
        scratch_shapes=[pltpu.VMEM((half, lat), BF16), dma(3 + ENC_CHUNKS)],
        compiler_params=pltpu.CompilerParams(vmem_limit_bytes=16 << 20),
        name="crosscoder_finish",
    )(*staged)


def solution(mesh):
    in_specs = (
        P("layer", ("latent", "dp"), None),
        P("layer", None, "latent"),
        P("layer", "latent", None),
        P("latent"),
        P("layer", None),
        P("latent", None, None),
        P("latent", None),
    )
    out_specs = (
        P("layer", "dp", "latent"),
        P("layer", "latent", "dp"),
        P(("latent", "dp")),
        P("layer", "dp"),
    )
    return jax.shard_map(
        on_device, mesh=mesh, in_specs=in_specs, out_specs=out_specs, check_vma=False
    )
```

```python
import functools
import math

import jax
import jax.numpy as jnp
from jax import lax
from jax.experimental import pallas as pl
from jax.experimental.pallas import tpu as pltpu
from jax.sharding import PartitionSpec as P

SPARSITY = 0.5
NORM_EPS = 1e-06
MESH = pl.DeviceIdType.MESH
F32 = jnp.float32
BF16 = jnp.bfloat16
ENC_CHUNKS = 4
CORES = 2


def chip_peers_of(chip, chips):
    if chips & (chips - 1):
        return [lax.rem(chip + k, chips) for k in range(1, chips)]
    peers = []
    for k in sorted(range(1, chips), key=lambda k: (-bin(k).count("1"), -k)):
        peer = chip
        for b in range(chips.bit_length() - 1):
            if k >> b & 1:
                peer = peer + (1 << b) - (2 << b) * lax.rem(chip // (1 << b), 2)
        peers.append(peer)
    return peers


def step_kernel(
    n_layer, n_lat, n_dp,
    acts_hbm, enc_hbm, dec_hbm, ebias_hbm, dbias_hbm, ids_hbm, counts_hbm,
    acts_t, pg_out, dec_stage, eb_stage, db_stage,
    acts_all, enc_v, dec_v, ebias_v, dbias_v, ids_v, counts_v,
    dec_t, acts_half, pre_send, pre_recv, codes_send, codes_recv,
    part_send, pair_recv, chip_send, part_recv, err_all, err_half, grad_send, grad_recv,
    gate_send, gate_recv,
    in_sems, send_sem, acts_rs, ahalf_rs, pre_rs, codes_rs,
    pair_rs, part_rs, err_rs, ehalf_rs, grad_rs, gate_rs,
):
    layer = lax.axis_index("layer")
    me = lax.axis_index("latent")
    group = lax.axis_index("dp")
    rows = acts_all.shape[1]
    width = acts_all.shape[2]
    lat = enc_v.shape[1]
    blocks, tiles = ids_v.shape
    rows_group = rows * n_lat
    half = width // n_dp
    lat_part = lat // n_dp
    scale = 1.0 / math.sqrt(rows_group * n_dp)

    chips = n_lat // CORES
    chip = me // CORES
    core = lax.rem(me, CORES)
    partner = chip * CORES + 1 - core
    chip_peers = chip_peers_of(chip, chips)
    n_peers = len(chip_peers)
    lat_peers = [lax.rem(me + k, n_lat) for k in range(1, n_lat)]
    layer_peers = [lax.rem(layer + k, n_layer) for k in range(1, n_layer)]
    dp_peers = [lax.rem(group + k, n_dp) for k in range(1, n_dp)]
    n_z = n_layer * n_dp
    rank = layer * n_dp + group
    others = [i + lax.div(i - rank + n_z, n_z) for i in range(n_z - 1)]
    z_peers = [(lax.div(i, n_dp), lax.rem(i, n_dp)) for i in others]

    own_acts = pltpu.make_async_copy(acts_hbm.at[0], acts_all.at[me], in_sems.at[0])
    own_acts.start()
    loads = [
        pltpu.make_async_copy(src, dst, in_sems.at[1])
        for _, (src, dst) in enumerate(
            (
                (enc_hbm.at[0], enc_v),
                (dec_hbm.at[0], dec_v),
                (ebias_hbm, ebias_v),
                (dbias_hbm, dbias_v),
                (ids_hbm.at[0], ids_v),
                (counts_hbm, counts_v),
            )
        )
    ]
    for load in loads:
        load.start()

    barrier = pltpu.get_barrier_semaphore()
    for p in lat_peers:
        pl.semaphore_signal(barrier, inc=1, device_id={"latent": p}, device_id_type=MESH)
    for p in layer_peers:
        pl.semaphore_signal(barrier, inc=1, device_id={"layer": p}, device_id_type=MESH)
    for p in dp_peers:
        pl.semaphore_signal(barrier, inc=1, device_id={"dp": p}, device_id_type=MESH)
    with jax.named_scope("entry"):
        pl.semaphore_wait(barrier, n_lat + n_layer + n_dp - 3)

    def remote(src, dst, rs, axis, peer):
        return pltpu.make_async_remote_copy(
            src_ref=src, dst_ref=dst, send_sem=send_sem.at[0], recv_sem=rs,
            device_id={axis: peer}, device_id_type=MESH,
        )

    sent = []

    def send(*args):
        copy = remote(*args)
        copy.start()
        sent.append(copy)

    def share(buf, rs):
        mine = buf.at[me]
        targets = [q * CORES + 1 - core for q in chip_peers] + [partner]
        for k, j in enumerate(targets):
            send(mine, mine, rs.at[me], "latent", j)

    def wait_block(buf, rs, j):
        remote(buf.at[j], buf.at[j], rs.at[j], "latent", partner).wait_recv()

    def gather(buf, rs, beside):
        for k, q in enumerate(chip_peers):
            j = q * CORES + 1 - core
            with jax.named_scope("relay"):
                wait_block(buf, rs, j)
            send(buf.at[j], buf.at[j], rs.at[j], "latent", partner)
        beside()
        with jax.named_scope("direct"):
            for j in [partner]:
                wait_block(buf, rs, j)
        with jax.named_scope("relayed"):
            for q in chip_peers:
                wait_block(buf, rs, q * CORES + core)
        return buf[...].astype(F32).reshape(rows_group, width).astype(BF16)

    def cross(src, dst_half, rs):
        for q, p in enumerate(dp_peers):
            cols = pl.ds(pl.multiple_of(p * half, 128), half)
            send(src.at[:, cols], dst_half.at[group, me], rs.at[group, 0], "dp", p)

    own_acts.wait()
    share(acts_all, acts_rs)
    cross(acts_all.at[me], acts_half, ahalf_rs)

    for load in loads:
        load.wait()
    dec_f = dec_v[...].astype(F32)
    norm_col = jnp.sqrt(jnp.sum(dec_f * dec_f, axis=1, keepdims=True) + NORM_EPS)
    r_i = lax.broadcasted_iota(jnp.int32, (lat, lat), 0)
    c_i = lax.broadcasted_iota(jnp.int32, (lat, lat), 1)
    norm_row = jnp.sum(
        jnp.where(r_i == c_i, jnp.broadcast_to(norm_col, (lat, lat)), 0.0), axis=0, keepdims=True
    )
    dec_t[...] = dec_v[...].T
    ids_i = ids_v[...]
    counts_i = counts_v[...]
    lat_block = lax.broadcasted_iota(jnp.int32, (rows_group, lat), 1) // (lat // blocks)
    pick_r = lax.broadcasted_iota(jnp.int32, (rows_group, tiles), 0) // rows
    pick_c = lax.broadcasted_iota(jnp.int32, (rows_group, tiles), 1)
    picked = pick_c == pick_r * n_dp + group
    mask = jnp.zeros((rows_group, lat), F32)
    for b in range(blocks):
        hit = jnp.zeros((1, tiles), F32)
        for k in range(blocks):
            hit = jnp.where((ids_i[k : k + 1, :] == b) & (counts_i > k), 1.0, hit)
        row_hit = jnp.sum(
            jnp.where(picked, jnp.broadcast_to(hit, (rows_group, tiles)), 0.0), axis=1, keepdims=True
        )
        mask = jnp.where(lat_block == b, jnp.broadcast_to(row_hit, (rows_group, lat)), mask)

    def wait_halves(dst_half, rs, p):
        blocks_in = dst_half.at[p, pl.ds(0, n_lat - 1)]
        remote(blocks_in, blocks_in, rs.at[p, 1], "latent", lat_peers[0]).wait_recv()

    def spread(dst_half, rs):
        for q, p in enumerate(dp_peers):
            with jax.named_scope("half"):
                remote(
                    dst_half.at[p, me], dst_half.at[p, me], rs.at[p, 0], "dp", p
                ).wait_recv()
            for k, j in enumerate(lat_peers):
                send(dst_half.at[p, me], dst_half.at[p, me], rs.at[p, 1], "latent", j)

    gathered = gather(acts_all, acts_rs, lambda: None)
    pre = jnp.dot(gathered, enc_v[...], preferred_element_type=F32)
    pre_send[...] = pre.astype(BF16)
    for k, p in enumerate(layer_peers):
        send(pre_send, pre_recv.at[layer], pre_rs.at[layer], "layer", p)
    spread(acts_half, ahalf_rs)
    pre = pre + ebias_v[...][None, :]
    for k, p in enumerate(layer_peers):
        with jax.named_scope("layers"):
            remote(pre_send, pre_recv.at[p], pre_rs.at[p], "layer", p).wait_recv()
        pre = pre + pre_recv[p].astype(F32)

    codes = (jax.nn.softplus(pre) * mask).astype(BF16)
    codes_send[...] = codes
    part = jnp.dot(codes, dec_v[...], preferred_element_type=F32)
    part_send[...] = part.reshape(n_lat, rows, width).astype(BF16)
    for k, q in enumerate(chip_peers):
        send(
            part_send.at[q * CORES + core], pair_recv.at[k],
            pair_rs.at[k], "latent", partner,
        )
    for k, j in enumerate([partner]):
        send(part_send.at[j], part_recv.at[me], part_rs.at[me], "latent", j)
    for k, q in enumerate(chip_peers):
        with jax.named_scope("pair"):
            remote(
                pair_recv.at[k], pair_recv.at[k], pair_rs.at[k], "latent", partner
            ).wait_recv()
        total = part_send[q * CORES + 1 - core].astype(F32) + pair_recv[k].astype(F32)
        chip_send[k] = total.astype(BF16)
        send(
            chip_send.at[k], part_recv.at[me], part_rs.at[me],
            "latent", q * CORES + 1 - core,
        )
    for k, p in enumerate(dp_peers):
        send(codes_send, codes_recv.at[group], codes_rs.at[group], "dp", p)

    mine_cols = pl.ds(pl.multiple_of(group * half, 128), half)
    acts_rows = [acts_all[:, :, mine_cols].astype(F32).reshape(rows_group, half)]
    for q, p in enumerate(dp_peers):
        with jax.named_scope("halves"):
            wait_halves(acts_half, ahalf_rs, p)
        acts_rows.append(acts_half[p].astype(F32).reshape(rows_group, half))
    acts_t[...] = jnp.concatenate(acts_rows, axis=0).T.astype(BF16)

    gate = mask * jax.nn.sigmoid(pre)
    gate_send[...] = gate.astype(BF16)
    for k, p in enumerate(dp_peers):
        send(gate_send, gate_recv.at[group], gate_rs.at[group], "dp", p)

    recon = part_send[me].astype(F32) + dbias_v[...]
    for j in [partner] + [q * CORES + 1 - core for q in chip_peers]:
        with jax.named_scope("chips"):
            wait_block(part_recv, part_rs, j)
        recon = recon + part_recv[j].astype(F32)
    err_all[me] = (scale * (recon - acts_all[me].astype(F32))).astype(BF16)
    share(err_all, err_rs)
    cross(err_all.at[me], err_half, ehalf_rs)

    code_rows = [codes.astype(F32)]
    for k, p in enumerate(dp_peers):
        remote(codes_send, codes_recv.at[p], codes_rs.at[p], "dp", p).wait_recv()
        code_rows.append(codes_recv[p].astype(F32))
    codes_t = jnp.concatenate(code_rows, axis=0).T
    totals = jnp.sum(codes_t, axis=1, keepdims=True)
    unit_gain = SPARSITY * scale * totals / norm_col
    codes_t = codes_t.astype(BF16)

    err = gather(err_all, err_rs, lambda: spread(err_half, ehalf_rs))
    grad = jnp.dot(err, dec_t[...], preferred_element_type=F32)
    grad = grad + SPARSITY * scale * norm_row
    grad_send[...] = grad.astype(BF16)
    gates = [gate]
    for k, d in enumerate(dp_peers):
        remote(gate_send, gate_recv.at[d], gate_rs.at[d], "dp", d).wait_recv()
        gates.append(gate_recv[d].astype(F32))
    for k, (p, d) in enumerate(z_peers):
        copy = pltpu.make_async_remote_copy(
            src_ref=grad_send, dst_ref=grad_recv.at[layer, group],
            send_sem=send_sem.at[0], recv_sem=grad_rs.at[layer, group],
            device_id={"layer": p, "dp": d}, device_id_type=MESH,
        )
        copy.start()
        sent.append(copy)

    err_rows = [err_all[:, :, mine_cols].astype(F32).reshape(rows_group, half)]
    for q, p in enumerate(dp_peers):
        with jax.named_scope("halves"):
            wait_halves(err_half, ehalf_rs, p)
        err_rows.append(err_half[p].astype(F32).reshape(rows_group, half))
    err_rows = jnp.concatenate(err_rows, axis=0)
    db_stage[...] = jnp.sum(err_rows, axis=0, keepdims=True)
    dec_grad = jnp.dot(codes_t, err_rows.astype(BF16), preferred_element_type=F32)
    dec_grad = dec_grad + unit_gain * dec_v[:, mine_cols].astype(F32)
    dec_stage[...] = dec_grad.astype(BF16)

    def wait_grad(p, d):
        with jax.named_scope("zgrad"):
          remote(grad_send, grad_recv.at[p, d], grad_rs.at[p, d], "latent", partner).wait_recv()
        return grad_recv[p, d].astype(F32)

    for p in layer_peers:
        grad = grad + wait_grad(p, group)
    pg_rows = [(grad * gates[0]).astype(BF16)]
    for k, d in enumerate(dp_peers):
        other = wait_grad(layer, d)
        for p in layer_peers:
            other = other + wait_grad(p, d)
        pg_rows.append((other * gates[k + 1]).astype(BF16))
    pg_rows = jnp.concatenate(pg_rows, axis=0)
    pg_out[...] = pg_rows
    bias_sum = jnp.sum(pg_rows.astype(F32), axis=0, keepdims=True)
    bias_mine = bias_sum[:, :lat_part]
    for d in range(1, n_dp):
        bias_mine = jnp.where(group == d, bias_sum[:, d * lat_part : (d + 1) * lat_part], bias_mine)
    eb_stage[...] = bias_mine.reshape(lat_part)
    with jax.named_scope("sends"):
      for copy in sent:
        copy.wait_send()


def finish_kernel(
    acts_t, pg_rows, dec_grad, eb_grad, db_grad, enc_out, dec_out, eb_out, db_out, enc_stage, sems
):
    copies = [
        pltpu.make_async_copy(dec_grad, dec_out.at[0], sems.at[0]),
        pltpu.make_async_copy(eb_grad, eb_out, sems.at[1]),
        pltpu.make_async_copy(db_grad, db_out, sems.at[2]),
    ]
    for copy in copies:
        copy.start()
    size = acts_t.shape[0] // ENC_CHUNKS
    for c in range(ENC_CHUNKS):
        part = pl.ds(c * size, size)
        enc_stage[part, :] = jnp.dot(
            acts_t[part, :], pg_rows[...], preferred_element_type=F32
        ).astype(BF16)
        copy = pltpu.make_async_copy(enc_stage.at[part, :], enc_out.at[0, part, :], sems.at[3 + c])
        copy.start()
        copies.append(copy)
    for copy in copies:
        copy.wait()


def on_device(layer_acts, enc_weight, dec_weight, enc_bias, dec_bias, block_ids, block_counts):
    n_layer = lax.axis_size("layer")
    n_lat = lax.axis_size("latent")
    n_dp = lax.axis_size("dp")
    rows, width = layer_acts.shape[1:]
    lat = enc_weight.shape[2]
    tiles, blocks = block_ids.shape[1:]
    group_rows = rows * n_lat
    chips = n_lat // CORES
    half = width // n_dp
    any_spec = pl.BlockSpec(memory_space=pltpu.HBM)
    vmem_spec = pl.BlockSpec(memory_space=pltpu.VMEM)
    dma = lambda *shape: pltpu.SemaphoreType.DMA(shape)
    staged = pl.pallas_call(
        functools.partial(step_kernel, n_layer, n_lat, n_dp),
        out_shape=(
            pltpu.VMEM((half, n_dp * group_rows), BF16),
            pltpu.VMEM((n_dp * group_rows, lat), BF16),
            pltpu.VMEM((lat, half), BF16),
            pltpu.VMEM((lat // n_dp,), F32),
            pltpu.VMEM((1, half), F32),
        ),
        in_specs=[any_spec] * 7,
        out_specs=(vmem_spec,) * 5,
        scratch_shapes=[
            pltpu.VMEM((n_lat, rows, width), BF16),
            pltpu.VMEM((width, lat), BF16),
            pltpu.VMEM((lat, width), BF16),
            pltpu.VMEM((lat,), F32),
            pltpu.VMEM((1, width), F32),
            pltpu.VMEM((blocks, tiles), jnp.int32),
            pltpu.VMEM((1, tiles), jnp.int32),
            pltpu.VMEM((width, lat), BF16),
            pltpu.VMEM((n_dp, n_lat, rows, half), BF16),
            pltpu.VMEM((group_rows, lat), BF16),
            pltpu.VMEM((n_layer, group_rows, lat), BF16),
            pltpu.VMEM((group_rows, lat), BF16),
            pltpu.VMEM((n_dp, group_rows, lat), BF16),
            pltpu.VMEM((n_lat, rows, width), BF16),
            pltpu.VMEM((chips, rows, width), BF16),
            pltpu.VMEM((chips, rows, width), BF16),
            pltpu.VMEM((n_lat, rows, width), BF16),
            pltpu.VMEM((n_lat, rows, width), BF16),
            pltpu.VMEM((n_dp, n_lat, rows, half), BF16),
            pltpu.VMEM((group_rows, lat), BF16),
            pltpu.VMEM((n_layer, n_dp, group_rows, lat), BF16),
            pltpu.VMEM((group_rows, lat), BF16),
            pltpu.VMEM((n_dp, group_rows, lat), BF16),
            dma(2), dma(1),
            dma(n_lat), dma(n_dp, 2), dma(n_layer), dma(n_dp),
            dma(chips), dma(n_lat), dma(n_lat), dma(n_dp, 2),
            dma(n_layer, n_dp), dma(n_dp),
        ],
        compiler_params=pltpu.CompilerParams(
            collective_id=0, has_side_effects=True, vmem_limit_bytes=40 << 20
        ),
        name="crosscoder_step",
    )(*[
        pltpu.with_memory_space_constraint(x, pltpu.HBM)
        for x in (
            layer_acts, enc_weight, dec_weight, enc_bias, dec_bias,
            jnp.swapaxes(block_ids, 1, 2), block_counts,
        )
    ])
    return pl.pallas_call(
        finish_kernel,
        out_shape=(
            jax.ShapeDtypeStruct((1, half, lat), BF16),
            jax.ShapeDtypeStruct((1, lat, half), BF16),
            jax.ShapeDtypeStruct((lat // n_dp,), F32),
            jax.ShapeDtypeStruct((1, half), F32),
        ),
        in_specs=[vmem_spec] * 5,
        out_specs=(any_spec,) * 4,
        scratch_shapes=[pltpu.VMEM((half, lat), BF16), dma(3 + ENC_CHUNKS)],
        compiler_params=pltpu.CompilerParams(vmem_limit_bytes=16 << 20),
        name="crosscoder_finish",
    )(*staged)


def solution(mesh):
    in_specs = (
        P("layer", ("latent", "dp"), None),
        P("layer", None, "latent"),
        P("layer", "latent", None),
        P("latent"),
        P("layer", None),
        P("latent", None, None),
        P("latent", None),
    )
    out_specs = (
        P("layer", "dp", "latent"),
        P("layer", "latent", "dp"),
        P(("latent", "dp")),
        P("layer", "dp"),
    )
    return jax.shard_map(
        on_device, mesh=mesh, in_specs=in_specs, out_specs=out_specs, check_vma=False
    )
```
